512 devices in a mesh: graph: 16 (over y, z_lo), gr: 4 (over z_hi), gc: 8 (over x, core).
Axes of the slice: x: 4, y: 8, z: 8 (z_hi: 4, z_lo: 2; z = z_hi * 2 + z_lo), core: 2. Of those that a mesh axis runs over, the one named last changes fastest.
Arguments:
- x_in: bfloat16 [8192, 256], P(('graph', 'gr', 'gc')), parts along dimension 0, may hold values from -64 to 64
- node_type: int32 [8192], P(('graph', 'gr', 'gc')), parts along dimension 0, may hold values from 0 to 7
- node_mask: int32 [8192], P(('graph', 'gr', 'gc')), parts along dimension 0, may hold values 0 or 1
- adj_cat: int32 [8192, 512], P(('graph', 'gc'), 'gr'), parts along dimension 0, may hold values from 0 to 4
- ori_cat: int32 [8192, 512], P(('graph', 'gc'), 'gr'), parts along dimension 0, may hold values from 0 to 7
- type_table: float32 [8, 256], replicated, may hold values from -6 to 6
- adj_table: float32 [5, 32], replicated, may hold values from -6 to 6
- ori_table: float32 [8, 32], replicated, may hold values from -6 to 6
- w_qkv: bfloat16 [256, 768], replicated, may hold values from -1.5 to 1.5
- w_film: bfloat16 [32, 512], replicated, may hold values from -0.75 to 0.75
- w_edge_out: bfloat16 [256, 32], replicated, may hold values from -0.375 to 0.375
- w_node_out: bfloat16 [256, 256], replicated, may hold values from -0.375 to 0.375
- w_node_up: bfloat16 [256, 512], replicated, may hold values from -0.375 to 0.375
- w_node_down: bfloat16 [512, 256], replicated, may hold values from -0.25 to 0.25
- w_edge_up: bfloat16 [32, 128], replicated, may hold values from -1 to 1
- w_edge_down: bfloat16 [128, 32], replicated, may hold values from -0.5 to 0.5
- node_gain1: float32 [256], replicated, may hold values from 0.25 to 1.75
- node_gain2: float32 [256], replicated, may hold values from 0.25 to 1.75
- edge_gain1: float32 [32], replicated, may hold values from 0.25 to 1.75
- edge_gain2: float32 [32], replicated, may hold values from 0.25 to 1.75
Outputs:
- node_out: bfloat16 [8192, 256], P(('graph', 'gr', 'gc')), parts along dimension 0
- edge_out: bfloat16 [32, 8192, 512], P(None, ('graph', 'gc'), 'gr'), parts along dimension 1
The draws below stay inside these ranges and needn't reach their ends.
There are 16 independent parts, one for each index of `graph`. The reference program is written for one: setup_inputs(seed, part) draws one part's arguments, and reference() takes and returns one part's arrays. A program takes and returns all parts, laid end to end along the dimension named above; an argument that names none is the same for every part. Nothing has to cross between parts.
All inputs are finite; a program needn't handle non-finite values. No bound on the sum of `node_mask` on one device may be relied on, other than what follows from the above.
Results may differ from the reference program's by a relative error of at most 0.0075.
The reference program's roundings to bfloat16 on the way count: a program that leaves them out, or rounds other values in their place, can miss the bound.
Values may be sent and summed in bfloat16 or wider, within the bound.
A program may use at most 64 MiB of HBM per device.

```python
import math
import jax
import jax.numpy as jnp
from jax import lax

NODES = 512
DX = 256
HEAD_DIM = 32
DE = 32
FFX = 512
FFE = 128
NTYPES = 8
ADJ = 5
ORI = 8


def draw_x_in(key, part):
    base = jnp.clip(jax.random.normal(jax.random.fold_in(key, 11), (NODES, DX), jnp.float32), -6.0, 6.0)
    return base.astype(jnp.bfloat16)


def with_ends(values, rng, low, high):
    longest = values.shape.index(max(values.shape))
    spots = []
    for shift in (0, 1):
        where = [jax.random.randint(jax.random.fold_in(rng, axis), (), 0, length) for axis, length in enumerate(values.shape)]
        where[longest] = (where[longest] + shift) % values.shape[longest]
        spots.append(tuple(where))
    return values.at[spots[0]].set(low).at[spots[1]].set(high)


def normal_values(own_key, dims, scale, reach, held_as=jnp.bfloat16):
    return jnp.clip(scale * jax.random.normal(own_key, dims, jnp.float32), -reach, reach).astype(held_as)


def setup_inputs(seed: int = 0, part: int = 0) -> dict:
    arg_keys = jax.random.split(jax.random.key(seed), 21)
    own_keys = jax.random.split(jax.random.fold_in(arg_keys[20], part), 21)
    return {
        "x_in": draw_x_in(jax.random.fold_in(jax.random.fold_in(arg_keys[20], part), 71), part),
        "node_type": with_ends(jax.random.randint(own_keys[1], (NODES,), 0, NTYPES), jax.random.fold_in(own_keys[1], 1), 0, NTYPES - 1).astype(jnp.int32),
        "node_mask": with_ends((jax.random.randint(own_keys[2], (NODES,), 0, 8) < 7).astype(jnp.int32), jax.random.fold_in(own_keys[2], 1), 0, 1),
        "adj_cat": with_ends(jax.random.randint(own_keys[3], (NODES, NODES), 0, ADJ), jax.random.fold_in(own_keys[3], 1), 0, ADJ - 1).astype(jnp.int32),
        "ori_cat": with_ends(jax.random.randint(own_keys[4], (NODES, NODES), 0, ORI), jax.random.fold_in(own_keys[4], 1), 0, ORI - 1).astype(jnp.int32),
        "type_table": normal_values(arg_keys[5], (NTYPES, DX), 1.0, 6.0, jnp.float32),
        "adj_table": normal_values(arg_keys[6], (ADJ, DE), 1.0, 6.0, jnp.float32),
        "ori_table": normal_values(arg_keys[7], (ORI, DE), 1.0, 6.0, jnp.float32),
        "w_qkv": normal_values(arg_keys[8], (DX, 3 * DX), (DX // 16) ** -0.5, 1.5),
        "w_film": normal_values(arg_keys[9], (DE, 2 * DX), (2 * DE) ** -0.5, 0.75),
        "w_edge_out": normal_values(arg_keys[10], (DX, DE), DX ** -0.5, 0.375),
        "w_node_out": normal_values(arg_keys[11], (DX, DX), DX ** -0.5, 0.375),
        "w_node_up": normal_values(arg_keys[12], (DX, FFX), DX ** -0.5, 0.375),
        "w_node_down": normal_values(arg_keys[13], (FFX, DX), FFX ** -0.5, 0.25),
        "w_edge_up": normal_values(arg_keys[14], (DE, FFE), DE ** -0.5, 1.0),
        "w_edge_down": normal_values(arg_keys[15], (FFE, DE), FFE ** -0.5, 0.5),
        "node_gain1": jnp.clip(1.0 + 0.15 * jax.random.normal(arg_keys[16], (DX,), jnp.float32), 0.25, 1.75),
        "node_gain2": jnp.clip(1.0 + 0.15 * jax.random.normal(arg_keys[17], (DX,), jnp.float32), 0.25, 1.75),
        "edge_gain1": jnp.clip(1.0 + 0.15 * jax.random.normal(arg_keys[18], (DE,), jnp.float32), 0.25, 1.75),
        "edge_gain2": jnp.clip(1.0 + 0.15 * jax.random.normal(arg_keys[19], (DE,), jnp.float32), 0.25, 1.75),
    }


def layer_norm(values, gain, axis):
    center = values - lax.optimization_barrier(jnp.mean(values, axis=axis, keepdims=True))
    spread = lax.optimization_barrier(jnp.mean(center * center, axis=axis, keepdims=True))
    return center / jnp.sqrt(spread + 1e-05) * gain

def round_bf16(values):
    return lax.optimization_barrier(values.astype(jnp.bfloat16)).astype(jnp.float32)

def wide_dot(left, right):
    return jnp.dot(left.astype(jnp.float32), right.astype(jnp.float32), precision=lax.Precision.HIGHEST)

def reference(x_in, node_type, node_mask, adj_cat, ori_cat, type_table, adj_table, ori_table, w_qkv, w_film, w_edge_out, w_node_out, w_node_up, w_node_down, w_edge_up, w_edge_down, node_gain1, node_gain2, edge_gain1, edge_gain2):
    nodes0 = (x_in.astype(jnp.float32) + type_table[node_type]).astype(jnp.bfloat16)
    projected = wide_dot(nodes0, w_qkv).astype(jnp.bfloat16)
    queries = projected[:, :DX].astype(jnp.float32)
    keys_all = projected[:, DX:2 * DX].astype(jnp.float32)
    values_all = projected[:, 2 * DX:].astype(jnp.float32)
    valid = node_mask.astype(jnp.float32)
    score_scale = 1.0 / math.sqrt(HEAD_DIM)
    width_block = min(64, NODES)
    film_weight = w_film.astype(jnp.float32)
    out_weight = w_edge_out.astype(jnp.float32)
    up_weight = w_edge_up.astype(jnp.float32)
    down_weight = w_edge_down.astype(jnp.float32)

    def one_block(begin_at):
        adj_part = lax.dynamic_slice_in_dim(adj_cat, begin_at, width_block, 1)
        ori_part = lax.dynamic_slice_in_dim(ori_cat, begin_at, width_block, 1)
        edges0 = (adj_table[adj_part] + ori_table[ori_part]).astype(jnp.bfloat16)
        edges0 = jnp.transpose(edges0, (2, 0, 1)).astype(jnp.float32)
        film = jnp.einsum('fjr,fk->kjr', edges0, film_weight, precision=lax.Precision.HIGHEST)
        query_part = lax.dynamic_slice_in_dim(queries, begin_at, width_block, 0)
        scores = keys_all.T[:, :, None] * query_part.T[:, None, :] * score_scale * (film[:DX] + 1.0) + film[DX:]
        message = jnp.einsum('cjr,cf->fjr', round_bf16(scores), out_weight, precision=lax.Precision.HIGHEST)
        masked = jnp.where(valid[None, :, None] > 0, scores, -1000000000.0)
        peak = lax.optimization_barrier(jnp.max(masked, axis=1, keepdims=True))
        expo = jnp.exp(masked - peak)
        attended = lax.optimization_barrier(jnp.sum(expo * values_all.T[:, :, None], axis=1)) / lax.optimization_barrier(jnp.sum(expo, axis=1))
        edges1 = round_bf16(layer_norm(edges0 + message, edge_gain1[:, None, None], 0))
        hidden_edge = round_bf16(jnp.maximum(jnp.einsum('fjr,fh->hjr', edges1, up_weight, precision=lax.Precision.HIGHEST), 0.0))
        edges2 = layer_norm(edges1 + jnp.einsum('hjr,hf->fjr', hidden_edge, down_weight, precision=lax.Precision.HIGHEST), edge_gain2[:, None, None], 0)
        row_valid = lax.dynamic_slice_in_dim(valid, begin_at, width_block, 0)
        edges2 = (edges2 * valid[None, :, None] * row_valid[None, None, :]).astype(jnp.bfloat16)
        return (attended.T, edges2)
    starts = jnp.arange(NODES // width_block, dtype=jnp.int32) * width_block
    attended, edge_blocks = lax.map(one_block, starts)
    attended = attended.reshape(NODES, DX)
    edge_out = jnp.transpose(edge_blocks, (1, 2, 0, 3)).reshape(DE, NODES, NODES)
    attn_bf = attended.astype(jnp.bfloat16)
    nodes1 = layer_norm(nodes0.astype(jnp.float32) + wide_dot(attn_bf, w_node_out), node_gain1, -1).astype(jnp.bfloat16)
    hidden_node = jnp.maximum(wide_dot(nodes1, w_node_up), 0.0).astype(jnp.bfloat16)
    node_out = (layer_norm(nodes1.astype(jnp.float32) + wide_dot(hidden_node, w_node_down), node_gain2, -1) * valid[:, None]).astype(jnp.bfloat16)
    return (node_out, edge_out)
```

```python
import functools
import math

import jax
import jax.numpy as jnp
from jax import lax
from jax.experimental import pallas as pl
from jax.experimental.pallas import tpu as pltpu
from jax.sharding import PartitionSpec as P

MESH = pl.DeviceIdType.MESH
F32, BF16 = jnp.float32, jnp.bfloat16
HEAD_DIM = 32
LOG2E = math.log2(math.e)
NEG = -1000000000.0
NT = (((1,), (1,)), ((), ()))


def dot(a, b):
    return jnp.dot(a, b, preferred_element_type=F32)


def dot_nt(a, b):
    return lax.dot_general(a, b, NT, preferred_element_type=F32)


def eye(n):
    rows = lax.broadcasted_iota(jnp.int32, (n, n), 0)
    cols = lax.broadcasted_iota(jnp.int32, (n, n), 1)
    return rows == cols


def norm(u, axis):
    center = u - jnp.mean(u, axis=axis, keepdims=True)
    spread = jnp.mean(center * center, axis=axis, keepdims=True)
    return center / jnp.sqrt(spread + 1e-05)


def kernel(
    x_h, type_s, mask_s, adj_h, ori_h, ttab_h, atab_h, otab_h, wqkv_h, wfilm_h,
    weo_h, wno_h, wnu_h, wnd_h, weu_h, wed_h, ng1_h, ng2_h, eg1_h, eg2_h,
    node_o, edge_o,
    x_v, adj_v, ori_v, ttab_v, atab_v, otab_v, wqkv_v, wfilm_v,
    weo_v, wno_v, wnu_v, wnd_v, weu_v, wed_v, ng1_v, ng2_v, eg1_v, eg2_v,
    node_v, edge_v,
    send, xq, xk, stat, rstat,
    t40, ft32, ftab, t40t, codes, onehot, film, score, e0, yrow,
    q_v, k_v, v_v, km_v, weot, weut, wedt, g1c, g2c,
    in_sem, out_sem, sendq, recvq, sendk, recvk, sends, recvs,
):
    gr, gc = lax.axis_index("gr"), lax.axis_index("gc")
    n_gr, n_gc = 4, 8

    pairs = [
        (x_h, x_v), (ttab_h, ttab_v), (adj_h, adj_v), (ori_h, ori_v),
        (atab_h, atab_v), (otab_h, otab_v), (wfilm_h, wfilm_v), (wqkv_h, wqkv_v),
        (weo_h, weo_v), (weu_h, weu_v), (wed_h, wed_v), (eg1_h, eg1_v), (eg2_h, eg2_v),
        (wno_h, wno_v), (wnu_h, wnu_v), (wnd_h, wnd_v), (ng1_h, ng1_v), (ng2_h, ng2_v),
    ]
    loads = [pltpu.make_async_copy(a, b, in_sem.at[i]) for i, (a, b) in enumerate(pairs)]

    barrier = pltpu.get_barrier_semaphore()
    far = lax.div(gc, 2) != gr
    for t in range(1, n_gc):
        pl.semaphore_signal(
            barrier, inc=1, device_id={"gc": lax.rem(gc + t, n_gc)}, device_id_type=MESH
        )

    @pl.when(far)
    def _():
        for t in range(4):
            pl.semaphore_signal(
                barrier, inc=1,
                device_id={"gr": lax.div(gc, 2), "gc": 4 * lax.rem(gc, 2) + t},
                device_id_type=MESH,
            )

    for copy in loads:
        copy.start()

    loads[0].wait()
    loads[1].wait()
    row_id = lax.broadcasted_iota(jnp.int32, (16, 256), 0)
    embedded = jnp.zeros((16, 256), F32)
    valid = jnp.zeros((16, 128), F32)
    for r in range(16):
        line = ttab_v[pl.ds(type_s[r], 1), :]
        embedded = jnp.where(row_id == r, line, embedded)
        valid = jnp.where(row_id[:, :128] == r, mask_s[r].astype(F32), valid)
    send[:, :256] = (x_v[...].astype(F32) + embedded).astype(BF16)
    send[:, 256:] = valid.astype(BF16)
    xq[pl.ds(gc, 1)] = send[...][None]

    def q_copy(peer, slot, index):
        return pltpu.make_async_remote_copy(
            src_ref=send, dst_ref=xq.at[slot], send_sem=sendq.at[index],
            recv_sem=recvq.at[slot], device_id={"gc": peer}, device_id_type=MESH,
        )

    def k_copy(peer, slot, index):
        return pltpu.make_async_remote_copy(
            src_ref=send, dst_ref=xk.at[slot], send_sem=sendk.at[index],
            recv_sem=recvk.at[slot],
            device_id={"gr": peer, "gc": 2 * gr + lax.div(gc, 4)}, device_id_type=MESH,
        )

    pl.semaphore_wait(barrier, n_gc - 1 + n_gr - 1)
    k_sent = [k_copy(lax.rem(gr + t, n_gr), lax.rem(gc, 4), t - 1) for t in (2, 1, 3)]
    q_sent = [q_copy(lax.rem(gc + t, n_gc), gc, t - 1) for t in (4, 3, 5, 2, 6, 1, 7)]
    for copy in k_sent + q_sent:
        copy.start()

    loads[4].wait()
    loads[5].wait()
    loads[6].wait()
    t40[...] = jnp.zeros_like(t40)
    ft32[...] = jnp.zeros_like(ft32)
    for a in range(5):
        t40[8 * a : 8 * a + 8, :32] = atab_v[a : a + 1, :] + otab_v[...]
    table = t40[...].astype(BF16)
    values = dot(table[:40, :32], wfilm_v[...])
    lane = lax.broadcasted_iota(jnp.int32, (40, 512), 1)
    values = values + jnp.where(lane < 256, 1.0, 0.0)
    high = values.astype(BF16).astype(F32)
    middle = (values - high).astype(BF16).astype(F32)
    ft32[0:40] = high
    ft32[40:80] = middle
    ft32[80:120] = values - high - middle
    ftab[...] = ft32[...].astype(BF16)
    t40t[...] = t40[...].T[:32].astype(BF16)

    loads[2].wait()
    loads[3].wait()
    code = (adj_v[...] * 8 + ori_v[...]).astype(F32)
    code_t = jnp.concatenate([code, code], axis=0).T
    for b in range(8):
        codes[b] = pltpu.roll(code_t, (128 - 8 * b) % 128, 1)
    lane = lax.broadcasted_iota(jnp.int32, (128, 128), 1)
    label = jnp.where(lane < 40, lane, jnp.where(lane < 80, lane - 40, lane - 80))
    label = jnp.where(lane < 120, label, -1).astype(F32)

    def film_block(b, carry):
        block = codes[b]
        for r in range(8):
            hit = jnp.broadcast_to(block[:, r : r + 1], (128, 128)) == label
            onehot[128 * r : 128 * r + 128] = jnp.where(hit, 1.0, 0.0).astype(BF16)
        hot = onehot[...]
        film[pl.ds(b * 8, 8)] = dot(hot, ftab[...]).reshape(8, 128, 512)
        e0[:, pl.ds(pl.multiple_of(b * 1024, 1024), 1024)] = dot_nt(t40t[...], hot)
        return carry

    lax.fori_loop(0, 8, film_block, 0)

    for i in range(7, 13):
        loads[i].wait()
    ident = jnp.where(eye(32), 1.0, 0.0).astype(BF16)
    weot[...] = dot_nt(ident, weo_v[...]).astype(BF16)
    wedt[...] = dot_nt(ident, wed_v[...]).astype(BF16)
    weut[...] = weu_v[...].astype(F32).T.astype(BF16)
    for g_ref, c_ref in ((eg1_v, g1c), (eg2_v, g2c)):
        spread = jnp.where(eye(32), jnp.broadcast_to(g_ref[...], (32, 32)), 0.0)
        c_ref[...] = jnp.broadcast_to(jnp.sum(spread, axis=1, keepdims=True), (32, 128))

    for t in range(1, n_gc):
        q_copy(gc, lax.rem(gc + t, n_gc), 0).wait_recv()
    nodes_q = xq[...].reshape(128, 384)
    q = dot(nodes_q[:, :256], wqkv_v[:, :256]).astype(BF16)
    q_v[...] = q.astype(F32) * (1.0 / math.sqrt(HEAD_DIM))
    row_mask = nodes_q[:, 256:].astype(F32).T[0:1, :]

    @pl.when(far)
    def _():
        for t in range(4):
            k_copy(gr, t, 0).wait_recv()

    @pl.when(jnp.logical_not(far))
    def _():
        xk[...] = xq[pl.ds(4 * lax.rem(gc, 2), 4)]

    nodes_k = xk[...].reshape(64, 384)
    kv = dot(nodes_k[:, :256], wqkv_v[:, 256:]).astype(BF16).astype(F32)
    k_v[...] = kv[:, :256]
    v_v[...] = kv[:, 256:]
    km_v[...] = nodes_k[:, 256:].astype(F32)

    def s_copy(owner, slot, index):
        return pltpu.make_async_remote_copy(
            src_ref=stat.at[owner], dst_ref=rstat.at[slot], send_sem=sends.at[index],
            recv_sem=recvs.at[slot], device_id={"gc": owner}, device_id_type=MESH,
        )

    def attend(t, carry):
        owner = lax.rem(gc + t + 1, n_gc)
        first = pl.multiple_of(owner * 16, 16)
        qs = q_v[pl.ds(first, 16), :]

        def peak_block(b, peak):
            for r in range(8):
                j = b * 8 + r
                live = jnp.broadcast_to(km_v[pl.ds(j, 1), :], (16, 128)) > 0
                live = jnp.concatenate([live, live], axis=1)
                k = jnp.broadcast_to(k_v[pl.ds(j, 1), :], (16, 256))
                s = k * qs * film[j, pl.ds(first, 16), :256] + film[j, pl.ds(first, 16), 256:]
                s = jnp.where(live, s, NEG)
                score[j, pl.ds(first, 16), :] = s
                peak = jnp.maximum(peak, s)
            return peak

        peak = lax.fori_loop(0, 8, peak_block, jnp.full((16, 256), -3e38, F32))

        def sum_block(b, state):
            total, weighted = state
            for r in range(8):
                j = b * 8 + r
                v = jnp.broadcast_to(v_v[pl.ds(j, 1), :], (16, 256))
                p = jnp.exp2((score[j, pl.ds(first, 16), :] - peak) * LOG2E)
                total = total + p
                weighted = weighted + p * v
            return total, weighted

        zero = jnp.zeros((16, 256), F32)
        total, weighted = lax.fori_loop(0, 8, sum_block, (zero, zero))
        stat[owner, 0] = peak
        stat[owner, 1] = total
        stat[owner, 2] = weighted

        @pl.when(t >= 1)
        def _():
            s_copy(lax.rem(gc + t, n_gc), gc, t - 1).start()

        return carry

    lax.fori_loop(0, n_gc, attend, 0)

    def edge_block(b, carry):
        for h in range(4):
            j = b * 16 + h * 4
            cols = pl.ds(pl.multiple_of(j * 128, 512), 512)
            sb = score[pl.ds(j, 4)].reshape(512, 256).astype(BF16)
            u = e0[:, cols] + dot_nt(weot[...], sb)
            gain = jnp.concatenate([g1c[...]] * 4, axis=1)
            e1 = (norm(u, 0) * gain).astype(BF16)
            hidden = jnp.maximum(dot(weut[...], e1), 0.0).astype(BF16)
            u = e1.astype(F32) + dot(wedt[...], hidden)
            gain = jnp.concatenate([g2c[...]] * 4, axis=1)
            y = norm(u, 0) * gain
            for r in range(4):
                yrow[pl.ds(h * 4 + r, 32, stride=16), :] = y[:, 128 * r : 128 * r + 128]
        keep = km_v[pl.ds(b * 16, 16), :] * row_mask
        edge_v[:, pl.ds(b * 16, 16), :] = (yrow[...].reshape(32, 16, 128) * keep[None]).astype(BF16)
        return carry

    lax.fori_loop(0, 4, edge_block, 0)
    out_edge = pltpu.make_async_copy(edge_v, edge_o, out_sem.at[0])
    out_edge.start()

    for i in range(13, 18):
        loads[i].wait()
    rstat[pl.ds(gc, 1)] = stat[pl.ds(gc, 1)]
    for t in range(1, n_gc):
        s_copy(gc, lax.rem(gc + t, n_gc), 0).wait_recv()
    peak = rstat[0, 0]
    for s in range(1, n_gc):
        peak = jnp.maximum(peak, rstat[s, 0])
    total = jnp.zeros((16, 256), F32)
    weighted = jnp.zeros((16, 256), F32)
    for s in range(n_gc):
        factor = jnp.exp2((rstat[s, 0] - peak) * LOG2E)
        total = total + rstat[s, 1] * factor
        weighted = weighted + rstat[s, 2] * factor
    attn = (weighted / total).astype(BF16)
    own = send[...].astype(F32)
    n1 = (norm(own[:, :256] + dot(attn, wno_v[...]), 1) * ng1_v[...]).astype(BF16)
    hid = jnp.maximum(dot(n1, wnu_v[...]), 0.0).astype(BF16)
    n2 = norm(n1.astype(F32) + dot(hid, wnd_v[...]), 1) * ng2_v[...]
    node_v[...] = (n2 * jnp.concatenate([own[:, 256:]] * 2, axis=1)).astype(BF16)
    out_node = pltpu.make_async_copy(node_v, node_o, out_sem.at[1])
    out_node.start()
    for copy in k_sent + q_sent:
        copy.wait_send()
    for t in range(n_gc - 1):
        s_copy(gc, gc, t).wait_send()
    out_edge.wait()
    out_node.wait()


def body(*args):
    (x_in, node_type, node_mask, adj, ori, ttab, atab, otab, wqkv, wfilm,
     weo, wno, wnu, wnd, weu, wed, ng1, ng2, eg1, eg2) = args
    args = (x_in, node_type, node_mask, adj, ori, ttab, atab, otab, wqkv, wfilm,
            weo, wno, wnu, wnd, weu, wed, ng1[None], ng2[None], eg1[None], eg2[None])
    anyspace = pl.BlockSpec(memory_space=pl.ANY)
    smem = pl.BlockSpec(memory_space=pltpu.SMEM)
    V = pltpu.VMEM
    D = pltpu.SemaphoreType.DMA
    loaded = [args[0]] + list(args[3:])
    return pl.pallas_call(
        kernel,
        out_shape=(
            jax.ShapeDtypeStruct((16, 256), BF16),
            jax.ShapeDtypeStruct((32, 64, 128), BF16),
        ),
        in_specs=[anyspace, smem, smem] + [anyspace] * 17,
        out_specs=(anyspace, anyspace),
        scratch_shapes=[V(a.shape, a.dtype) for a in loaded] + [
            V((16, 256), BF16),
            V((32, 64, 128), BF16),
            V((16, 384), BF16),
            V((8, 16, 384), BF16),
            V((4, 16, 384), BF16),
            V((8, 3, 16, 256), F32),
            V((8, 3, 16, 256), F32),
            V((128, 128), F32),
            V((128, 512), F32),
            V((128, 512), BF16),
            V((32, 128), BF16),
            V((8, 128, 128), F32),
            V((1024, 128), BF16),
            V((64, 128, 512), F32),
            V((64, 128, 256), F32),
            V((32, 8192), F32),
            V((512, 128), F32),
            V((128, 256), F32),
            V((64, 256), F32),
            V((64, 256), F32),
            V((64, 128), F32),
            V((32, 256), BF16),
            V((128, 32), BF16),
            V((32, 128), BF16),
            V((32, 128), F32),
            V((32, 128), F32),
            D((18,)), D((2,)), D((7,)), D((8,)), D((3,)), D((4,)), D((7,)), D((8,)),
        ],
        compiler_params=pltpu.CompilerParams(
            collective_id=0, has_side_effects=True, vmem_limit_bytes=60 * 1024 * 1024
        ),
    )(*args)


def solution(mesh):
    nodes = P(("graph", "gr", "gc"))
    rows = P(("graph", "gr", "gc"), None)
    pair = P(("graph", "gc"), "gr")
    return jax.shard_map(
        body,
        mesh=mesh,
        in_specs=(rows, nodes, nodes, pair, pair) + (P(),) * 15,
        out_specs=(rows, P(None, ("graph", "gc"), "gr")),
        check_vma=False,
    )
```

```python
import functools
import math

import jax
import jax.numpy as jnp
from jax import lax
from jax.experimental import pallas as pl
from jax.experimental.pallas import tpu as pltpu
from jax.sharding import PartitionSpec as P

MESH = pl.DeviceIdType.MESH
F32, BF16 = jnp.float32, jnp.bfloat16
HEAD_DIM = 32
LN2 = math.log(2.0)
LOG2E = math.log2(math.e)
NEG = -1000000000.0 * LOG2E
NT = (((1,), (1,)), ((), ()))


def dot(a, b):
    return jnp.dot(a, b, preferred_element_type=F32)


def dot_nt(a, b):
    return lax.dot_general(a, b, NT, preferred_element_type=F32)


def eye(n):
    rows = lax.broadcasted_iota(jnp.int32, (n, n), 0)
    cols = lax.broadcasted_iota(jnp.int32, (n, n), 1)
    return rows == cols


def norm(u, axis):
    center = u - jnp.mean(u, axis=axis, keepdims=True)
    spread = jnp.mean(center * center, axis=axis, keepdims=True)
    return center * lax.rsqrt(spread + 1e-05)


def kernel(
    x_h, type_h, mask_h, adj_h, ori_h, ttab_h, atab_h, otab_h, wqkv_h, wfilm_h,
    weo_h, wno_h, wnu_h, wnd_h, weu_h, wed_h, ng1_h, ng2_h, eg1_h, eg2_h,
    node_v, edge_v,
    type_s, mask_s,
    x_v, adj_v, ori_v, ttab_v, atab_v, otab_v, wqkv_v, wfilm_v,
    weo_v, wno_v, wnu_v, wnd_v, weu_v, wed_v, ng1_v, ng2_v, eg1_v, eg2_v,
    send, xq, xk, stat, rstat,
    t40, ft32, ftab, t40t, codes, onehot, film, score, e0, yrow,
    q_v, k_v, v_v, km_v, weut, g1c, g2c, u_s, e_s, h_s,
    in_sem, sendq, recvq, sendk, recvk, sends, recvs,
):
    gr, gc = lax.axis_index("gr"), lax.axis_index("gc")
    n_gr, n_gc = 4, 8

    barrier = pltpu.get_barrier_semaphore()
    home = lax.div(gc, 2)
    source = home == gr

    @pl.when(jnp.logical_not(source))
    def _():
        pl.semaphore_signal(barrier, inc=1, device_id={"gr": home}, device_id_type=MESH)

    for t in range(1, n_gc):
        pl.semaphore_signal(
            barrier, inc=1, device_id={"gc": lax.rem(gc + t, n_gc)}, device_id_type=MESH
        )
    pairs = [
        (x_h, x_v), (ttab_h, ttab_v), (adj_h, adj_v), (ori_h, ori_v),
        (atab_h, atab_v), (otab_h, otab_v), (wfilm_h, wfilm_v), (wqkv_h, wqkv_v),
        (weo_h, weo_v), (weu_h, weu_v), (wed_h, wed_v), (eg1_h, eg1_v), (eg2_h, eg2_v),
        (wno_h, wno_v), (wnu_h, wnu_v), (wnd_h, wnd_v), (ng1_h, ng1_v), (ng2_h, ng2_v),
        (type_h, type_s), (mask_h, mask_s),
    ]
    loads = [pltpu.make_async_copy(a, b, in_sem.at[i]) for i, (a, b) in enumerate(pairs)]
    for i in [18, 19] + list(range(18)):
        loads[i].start()

    for i in (18, 19, 0, 1):
        loads[i].wait()
    row_id = lax.broadcasted_iota(jnp.int32, (16, 256), 0)
    embedded = jnp.zeros((16, 256), F32)
    valid = jnp.zeros((16, 128), F32)
    for r in range(16):
        line = ttab_v[pl.ds(type_s[r], 1), :]
        embedded = jnp.where(row_id == r, line, embedded)
        valid = jnp.where(row_id[:, :128] == r, mask_s[r].astype(F32), valid)
    send[:, :256] = (x_v[...].astype(F32) + embedded).astype(BF16)
    send[:, 256:] = valid.astype(BF16)
    xq[pl.ds(gc, 1)] = send[...][None]

    def q_copy(peer, slot, index):
        return pltpu.make_async_remote_copy(
            src_ref=send, dst_ref=xq.at[slot], send_sem=sendq.at[index],
            recv_sem=recvq.at[slot], device_id={"gc": peer}, device_id_type=MESH,
        )

    def k_copy(peer, slot, index):
        return pltpu.make_async_remote_copy(
            src_ref=xq.at[4 * lax.rem(gc, 2) + slot], dst_ref=xk.at[slot], send_sem=sendk.at[index],
            recv_sem=recvk.at[slot], device_id={"gr": peer}, device_id_type=MESH,
        )

    @pl.when(source)
    def _():
        pl.semaphore_wait(barrier, n_gc - 1 + n_gr - 1)

    @pl.when(jnp.logical_not(source))
    def _():
        pl.semaphore_wait(barrier, n_gc - 1)

    q_sent = [q_copy(lax.rem(gc + t, n_gc), gc, t - 1) for t in (4, 3, 5, 2, 6, 1, 7)]
    for copy in q_sent:
        copy.start()
    for t in range(1, n_gc):
        @pl.when(source)
        def _():
            q_copy(gc, lax.rem(gc + t, n_gc), 0).wait_recv()

    @pl.when(source)
    def _():
        for t in (2, 1, 3):
            for slot in range(4):
                k_copy(lax.rem(gr + t, n_gr), slot, 3 * slot + t - 1).start()

    loads[4].wait()
    loads[5].wait()
    loads[6].wait()
    t40[...] = jnp.zeros_like(t40)
    ft32[...] = jnp.zeros_like(ft32)
    for a in range(5):
        t40[8 * a : 8 * a + 8, :32] = atab_v[a : a + 1, :] + otab_v[...]
    table = t40[...].astype(BF16)
    values = dot(table[:40, :32], wfilm_v[...])
    lane = lax.broadcasted_iota(jnp.int32, (40, 512), 1)
    values = values + jnp.where(lane < 256, 1.0, 0.0)
    values = values * LOG2E
    high = values.astype(BF16).astype(F32)
    middle = (values - high).astype(BF16).astype(F32)
    ft32[0:40] = high
    ft32[40:80] = middle
    ft32[80:120] = values - high - middle
    ftab[...] = ft32[...].astype(BF16)
    t40t[...] = t40[...].T[:32].astype(BF16)

    loads[2].wait()
    loads[3].wait()
    code = (adj_v[...] * 8 + ori_v[...]).astype(F32)
    code_t = jnp.concatenate([code, code], axis=0).T
    for b in range(8):
        codes[b] = pltpu.roll(code_t, (128 - 8 * b) % 128, 1)
    lane = lax.broadcasted_iota(jnp.int32, (128, 128), 1)
    label = jnp.where(lane < 40, lane, jnp.where(lane < 80, lane - 40, lane - 80))
    label = jnp.where(lane < 120, label, -1).astype(F32)

    for t in range(1, n_gc):
        @pl.when(jnp.logical_not(source))
        def _():
            q_copy(gc, lax.rem(gc + t, n_gc), 0).wait_recv()

    loads[7].wait()
    nodes_q = xq[...].reshape(128, 384)
    q = dot(nodes_q[:, :256], wqkv_v[:, :256]).astype(BF16)
    q_v[...] = q.astype(F32) * (1.0 / math.sqrt(HEAD_DIM))
    row_mask = nodes_q[:, 256:].astype(F32).T[0:1, :]

    def film_block(b, carry):
        block = codes[b]
        for r in range(8):
            hit = jnp.broadcast_to(block[:, r : r + 1], (128, 128)) == label
            onehot[128 * r : 128 * r + 128] = jnp.where(hit, 1.0, 0.0).astype(BF16)
        hot = onehot[...]
        film[pl.ds(b * 8, 8), :, :256] = dot(hot, ftab[:, :256]).reshape(8, 128, 256) * q_v[...][None]
        film[pl.ds(b * 8, 8), :, 256:] = dot(hot, ftab[:, 256:]).reshape(8, 128, 256)
        e0[:, pl.ds(pl.multiple_of(b * 1024, 1024), 1024)] = dot_nt(t40t[...], hot)
        return carry

    lax.fori_loop(0, 8, film_block, 0)

    for i in range(8, 13):
        loads[i].wait()
    weut[...] = weu_v[...].astype(F32).T.astype(BF16)
    for g_ref, c_ref in ((eg1_v, g1c), (eg2_v, g2c)):
        spread = jnp.where(eye(32), jnp.broadcast_to(g_ref[...], (32, 32)), 0.0)
        c_ref[...] = jnp.broadcast_to(jnp.sum(spread, axis=1, keepdims=True), (32, 128))

    @pl.when(jnp.logical_not(source))
    def _():
        for t in range(4):
            k_copy(gr, t, 0).wait_recv()

    @pl.when(source)
    def _():
        xk[...] = xq[pl.ds(4 * lax.rem(gc, 2), 4)]

    nodes_k = xk[...].reshape(64, 384)
    kv = dot(nodes_k[:, :256], wqkv_v[:, 256:]).astype(BF16).astype(F32)
    k_v[...] = kv[:, :256]
    v_v[...] = kv[:, 256:]
    km_v[...] = nodes_k[:, 256:].astype(F32)

    def s_copy(owner, slot, index):
        return pltpu.make_async_remote_copy(
            src_ref=stat.at[owner], dst_ref=rstat.at[slot], send_sem=sends.at[index],
            recv_sem=recvs.at[slot], device_id={"gc": owner}, device_id_type=MESH,
        )

    def owner_of(t):
        h = lax.div(t, 2)
        chip = lax.rem(lax.div(gc, 2) + 2 + h - lax.div(h, 2) * (2 * h - 1), 4)
        return 2 * chip + lax.rem(gc + t + 1, 2)

    def attend(t, carry):
        owner = owner_of(t)
        first = pl.multiple_of(owner * 16, 16)

        peak = jnp.full((16, 256), -3e38, F32)
        for j in range(64):
            live = jnp.broadcast_to(km_v[j : j + 1, :], (16, 128)) > 0
            live = jnp.concatenate([live, live], axis=1)
            k = jnp.broadcast_to(k_v[j : j + 1, :], (16, 256))
            s = k * film[j, pl.ds(first, 16), :256] + film[j, pl.ds(first, 16), 256:]
            s = jnp.where(live, s, NEG)
            score[j, pl.ds(first, 16), :] = s
            peak = jnp.maximum(peak, s)
        total = jnp.zeros((16, 256), F32)
        weighted = jnp.zeros((16, 256), F32)
        for j in range(64):
            v = jnp.broadcast_to(v_v[j : j + 1, :], (16, 256))
            p = jnp.exp2(score[j, pl.ds(first, 16), :] - peak)
            total = total + p
            weighted = weighted + p * v
        stat[owner, 0] = peak
        stat[owner, 1] = total
        stat[owner, 2] = weighted

        @pl.when(t >= 1)
        def _():
            s_copy(owner_of(t - 1), gc, t - 1).start()

        return carry

    lax.fori_loop(0, n_gc, attend, 0)

    gain1, gain2 = g1c[...], g2c[...]

    def message_stage(n):
        sb = (score[2 * n : 2 * n + 2].reshape(256, 256) * LN2).astype(BF16)
        u_s[n % 4] = e0[:, 256 * n : 256 * n + 256] + dot_nt(weo_v[...], sb)

    def norm_stage(n):
        for r in range(2):
            cols = slice(128 * r, 128 * r + 128)
            e_s[n % 8, :, cols] = (norm(u_s[n % 4, :, cols], 0) * gain1).astype(BF16)

    def up_stage(n):
        h_s[n % 4] = jnp.maximum(dot(weut[...], e_s[n % 8]).astype(BF16), 0.0)

    def down_stage(n):
        u = e_s[n % 8].astype(F32) + dot(wed_v[...], h_s[n % 4])
        for r in range(2):
            y = norm(u[:, 128 * r : 128 * r + 128], 0) * gain2
            yrow[(n // 8) % 2, pl.ds(2 * (n % 8) + r, 32, stride=16), :] = y
        if n % 8 == 7:
            at = 2 * n - 14
            keep = km_v[at : at + 16, :] * row_mask
            edge_v[:, at : at + 16, :] = (
                yrow[(n // 8) % 2].reshape(32, 16, 128) * keep[None]
            ).astype(BF16)

    for n in range(35):
        for lag, stage in enumerate((message_stage, norm_stage, up_stage, down_stage)):
            if 0 <= n - lag < 32:
                stage(n - lag)

    for i in range(13, 18):
        loads[i].wait()
    rstat[pl.ds(gc, 1)] = stat[pl.ds(gc, 1)]
    for t in range(1, n_gc):
        s_copy(gc, lax.rem(gc + t, n_gc), 0).wait_recv()
    peak = rstat[0, 0]
    for s in range(1, n_gc):
        peak = jnp.maximum(peak, rstat[s, 0])
    total = jnp.zeros((16, 256), F32)
    weighted = jnp.zeros((16, 256), F32)
    for s in range(n_gc):
        factor = jnp.exp2(rstat[s, 0] - peak)
        total = total + rstat[s, 1] * factor
        weighted = weighted + rstat[s, 2] * factor
    attn = (weighted / total).astype(BF16)
    own = send[...].astype(F32)
    n1 = (norm(own[:, :256] + dot(attn, wno_v[...]), 1) * ng1_v[...]).astype(BF16)
    hid = jnp.maximum(dot(n1, wnu_v[...]), 0.0).astype(BF16)
    n2 = norm(n1.astype(F32) + dot(hid, wnd_v[...]), 1) * ng2_v[...]
    node_v[...] = (n2 * jnp.concatenate([own[:, 256:]] * 2, axis=1)).astype(BF16)
    for copy in q_sent:
        copy.wait_send()

    @pl.when(source)
    def _():
        for t in range(12):
            k_copy(gr, 0, t).wait_send()

    for t in range(n_gc - 1):
        s_copy(gc, gc, t).wait_send()


def store(node_i, edge_i, node_o, edge_o, sem):
    copies = [
        pltpu.make_async_copy(edge_i, edge_o, sem.at[0]),
        pltpu.make_async_copy(node_i, node_o, sem.at[1]),
    ]
    for copy in copies:
        copy.start()
    for copy in copies:
        copy.wait()


def body(*args):
    (x_in, node_type, node_mask, adj, ori, ttab, atab, otab, wqkv, wfilm,
     weo, wno, wnu, wnd, weu, wed, ng1, ng2, eg1, eg2) = args
    args = (x_in, node_type, node_mask, adj, ori, ttab, atab, otab, wqkv, wfilm,
            weo.T, wno, wnu, wnd, weu, wed.T, ng1[None], ng2[None], eg1[None], eg2[None])
    anyspace = pl.BlockSpec(memory_space=pl.ANY)
    vmem = pl.BlockSpec(memory_space=pltpu.VMEM)
    hbm = pl.BlockSpec(memory_space=pltpu.HBM)
    V = pltpu.VMEM
    D = pltpu.SemaphoreType.DMA
    loaded = [args[0]] + list(args[3:])
    node, edge = pl.pallas_call(
        kernel,
        out_shape=(
            jax.ShapeDtypeStruct((16, 256), BF16),
            jax.ShapeDtypeStruct((32, 64, 128), BF16),
        ),
        in_specs=[hbm] * 20,
        out_specs=(vmem, vmem),
        scratch_shapes=[pltpu.SMEM((16,), jnp.int32)] * 2 + [V(a.shape, a.dtype) for a in loaded] + [
            V((16, 384), BF16),
            V((8, 16, 384), BF16),
            V((4, 16, 384), BF16),
            V((8, 3, 16, 256), F32),
            V((8, 3, 16, 256), F32),
            V((128, 128), F32),
            V((128, 512), F32),
            V((128, 512), BF16),
            V((32, 128), BF16),
            V((8, 128, 128), F32),
            V((1024, 128), BF16),
            V((64, 128, 512), F32),
            V((64, 128, 256), F32),
            V((32, 8192), F32),
            V((2, 512, 128), F32),
            V((128, 256), F32),
            V((64, 256), F32),
            V((64, 256), F32),
            V((64, 128), F32),
            V((128, 32), BF16),
            V((32, 128), F32),
            V((32, 128), F32),
            V((4, 32, 256), F32),
            V((8, 32, 256), BF16),
            V((4, 128, 256), BF16),
            D((20,)), D((7,)), D((8,)), D((12,)), D((4,)), D((7,)), D((8,)),
        ],
        compiler_params=pltpu.CompilerParams(
            collective_id=0, has_side_effects=True, vmem_limit_bytes=40 * 1024 * 1024
        ),
    )(*[pltpu.with_memory_space_constraint(a, pltpu.HBM) for a in args])
    return pl.pallas_call(
        store,
        out_shape=(
            jax.ShapeDtypeStruct((16, 256), BF16),
            jax.ShapeDtypeStruct((32, 64, 128), BF16),
        ),
        in_specs=[anyspace, anyspace],
        out_specs=(hbm, hbm),
        scratch_shapes=[D((2,))],
        compiler_params=pltpu.CompilerParams(vmem_limit_bytes=4 * 1024 * 1024),
    )(node, edge)


def solution(mesh):
    nodes = P(("graph", "gr", "gc"))
    rows = P(("graph", "gr", "gc"), None)
    pair = P(("graph", "gc"), "gr")
    return jax.shard_map(
        body,
        mesh=mesh,
        in_specs=(rows, nodes, nodes, pair, pair) + (P(),) * 15,
        out_specs=(rows, P(None, ("graph", "gc"), "gr")),
        check_vma=False,
    )
```

```python
import functools
import math

import jax
import jax.numpy as jnp
from jax import lax
from jax.experimental import pallas as pl
from jax.experimental.pallas import tpu as pltpu
from jax.sharding import PartitionSpec as P

MESH = pl.DeviceIdType.MESH
F32, BF16 = jnp.float32, jnp.bfloat16
HEAD_DIM = 32
LN2 = math.log(2.0)
LOG2E = math.log2(math.e)
NEG = -1000000000.0 * LOG2E
NT = (((1,), (1,)), ((), ()))


def dot(a, b):
    return jnp.dot(a, b, preferred_element_type=F32)


def dot_nt(a, b):
    return lax.dot_general(a, b, NT, preferred_element_type=F32)


def eye(n):
    rows = lax.broadcasted_iota(jnp.int32, (n, n), 0)
    cols = lax.broadcasted_iota(jnp.int32, (n, n), 1)
    return rows == cols


def norm(u, axis):
    center = u - jnp.mean(u, axis=axis, keepdims=True)
    spread = jnp.mean(center * center, axis=axis, keepdims=True)
    return center * lax.rsqrt(spread + 1e-05)


def kernel(
    x_h, type_h, mask_h, adj_h, ori_h, ttab_h, atab_h, otab_h, wqkv_h, wfilm_h,
    weo_h, wno_h, wnu_h, wnd_h, weu_h, wed_h, ng1_h, ng2_h, eg1_h, eg2_h,
    node_v, edge_v,
    type_s, mask_s,
    x_v, adj_v, ori_v, ttab_v, atab_v, otab_v, wqkv_v, wfilm_v,
    weo_v, wno_v, wnu_v, wnd_v, weu_v, wed_v, ng1_v, ng2_v, eg1_v, eg2_v,
    send, xq, xk, stat, rstat,
    t40, ft32, ftab, t40t, codes, onehot, film, score, e0, yrow,
    q_v, k_v, v_v, km_v, weut, g1c, g2c, u_s, e_s, h_s,
    in_sem, sendq, recvq, sendk, recvk, sends, recvs,
):
    gr, gc = lax.axis_index("gr"), lax.axis_index("gc")
    n_gr, n_gc = 4, 8

    barrier = pltpu.get_barrier_semaphore()
    home = lax.div(gc, 2)
    source = home == gr

    @pl.when(jnp.logical_not(source))
    def _():
        pl.semaphore_signal(barrier, inc=1, device_id={"gr": home}, device_id_type=MESH)

    for t in range(1, n_gc):
        pl.semaphore_signal(
            barrier, inc=1, device_id={"gc": lax.rem(gc + t, n_gc)}, device_id_type=MESH
        )
    pairs = [
        (x_h, x_v), (ttab_h, ttab_v), (adj_h, adj_v), (ori_h, ori_v),
        (atab_h, atab_v), (otab_h, otab_v), (wfilm_h, wfilm_v), (wqkv_h, wqkv_v),
        (weo_h, weo_v), (weu_h, weu_v), (wed_h, wed_v), (eg1_h, eg1_v), (eg2_h, eg2_v),
        (wno_h, wno_v), (wnu_h, wnu_v), (wnd_h, wnd_v), (ng1_h, ng1_v), (ng2_h, ng2_v),
        (type_h, type_s), (mask_h, mask_s),
    ]
    loads = [pltpu.make_async_copy(a, b, in_sem.at[i]) for i, (a, b) in enumerate(pairs)]
    for i in [18, 19] + list(range(18)):
        loads[i].start()

    for i in (18, 19, 0, 1):
        loads[i].wait()
    row_id = lax.broadcasted_iota(jnp.int32, (16, 256), 0)
    embedded = jnp.zeros((16, 256), F32)
    valid = jnp.zeros((16, 128), F32)
    for r in range(16):
        line = ttab_v[pl.ds(type_s[r], 1), :]
        embedded = jnp.where(row_id == r, line, embedded)
        valid = jnp.where(row_id[:, :128] == r, mask_s[r].astype(F32), valid)
    send[:, :256] = (x_v[...].astype(F32) + embedded).astype(BF16)
    send[:, 256:] = valid.astype(BF16)
    xq[pl.ds(gc, 1)] = send[...][None]

    def q_copy(peer, slot, index):
        return pltpu.make_async_remote_copy(
            src_ref=send, dst_ref=xq.at[slot], send_sem=sendq.at[index],
            recv_sem=recvq.at[slot], device_id={"gc": peer}, device_id_type=MESH,
        )

    def k_copy(peer, slot, index):
        return pltpu.make_async_remote_copy(
            src_ref=xq.at[4 * lax.rem(gc, 2) + slot], dst_ref=xk.at[slot], send_sem=sendk.at[index],
            recv_sem=recvk.at[slot], device_id={"gr": peer}, device_id_type=MESH,
        )

    @pl.when(source)
    def _():
        pl.semaphore_wait(barrier, n_gc - 1 + n_gr - 1)

    @pl.when(jnp.logical_not(source))
    def _():
        pl.semaphore_wait(barrier, n_gc - 1)

    q_sent = [q_copy(lax.rem(gc + t, n_gc), gc, t - 1) for t in (4, 3, 5, 2, 6, 1, 7)]
    for copy in q_sent:
        copy.start()
    for t in range(1, n_gc):
        @pl.when(source)
        def _():
            q_copy(gc, lax.rem(gc + t, n_gc), 0).wait_recv()

    @pl.when(source)
    def _():
        for t in (2, 1, 3):
            for slot in range(4):
                k_copy(lax.rem(gr + t, n_gr), slot, 3 * slot + t - 1).start()

    loads[4].wait()
    loads[5].wait()
    loads[6].wait()
    t40[...] = jnp.zeros_like(t40)
    ft32[...] = jnp.zeros_like(ft32)
    for a in range(5):
        t40[8 * a : 8 * a + 8, :32] = atab_v[a : a + 1, :] + otab_v[...]
    table = t40[...].astype(BF16)
    values = dot(table[:40, :32], wfilm_v[...])
    lane = lax.broadcasted_iota(jnp.int32, (40, 512), 1)
    values = values + jnp.where(lane < 256, 1.0, 0.0)
    values = values * LOG2E
    high = values.astype(BF16).astype(F32)
    middle = (values - high).astype(BF16).astype(F32)
    ft32[0:40] = high
    ft32[40:80] = middle
    ft32[80:120] = values - high - middle
    ftab[...] = ft32[...].astype(BF16)
    t40t[...] = t40[...].T[:32].astype(BF16)

    loads[2].wait()
    loads[3].wait()
    code = (adj_v[...] * 8 + ori_v[...]).astype(F32)
    code_t = jnp.concatenate([code, code], axis=0).T
    for b in range(8):
        codes[b] = pltpu.roll(code_t, (128 - 8 * b) % 128, 1)
    lane = lax.broadcasted_iota(jnp.int32, (128, 128), 1)
    label = jnp.where(lane < 40, lane, jnp.where(lane < 80, lane - 40, lane - 80))
    label = jnp.where(lane < 120, label, -1).astype(F32)

    for t in range(1, n_gc):
        @pl.when(jnp.logical_not(source))
        def _():
            q_copy(gc, lax.rem(gc + t, n_gc), 0).wait_recv()

    loads[7].wait()
    nodes_q = xq[...].reshape(128, 384)
    q = dot(nodes_q[:, :256], wqkv_v[:, :256]).astype(BF16)
    q_v[...] = q.astype(F32) * (1.0 / math.sqrt(HEAD_DIM))
    row_mask = nodes_q[:, 256:].astype(F32).T[0:1, :]

    def film_block(b, carry):
        block = codes[b]
        for r in range(8):
            hit = jnp.broadcast_to(block[:, r : r + 1], (128, 128)) == label
            onehot[128 * r : 128 * r + 128] = jnp.where(hit, 1.0, 0.0).astype(BF16)
        hot = onehot[...]
        film[pl.ds(b * 8, 8), :, :256] = dot(hot, ftab[:, :256]).reshape(8, 128, 256) * q_v[...][None]
        film[pl.ds(b * 8, 8), :, 256:] = dot(hot, ftab[:, 256:]).reshape(8, 128, 256)
        e0[:, pl.ds(pl.multiple_of(b * 1024, 1024), 1024)] = dot_nt(t40t[...], hot)
        return carry

    lax.fori_loop(0, 8, film_block, 0)

    for i in range(8, 13):
        loads[i].wait()
    weut[...] = weu_v[...].astype(F32).T.astype(BF16)
    for g_ref, c_ref in ((eg1_v, g1c), (eg2_v, g2c)):
        spread = jnp.where(eye(32), jnp.broadcast_to(g_ref[...], (32, 32)), 0.0)
        c_ref[...] = jnp.broadcast_to(jnp.sum(spread, axis=1, keepdims=True), (32, 128))

    @pl.when(jnp.logical_not(source))
    def _():
        for t in range(4):
            k_copy(gr, t, 0).wait_recv()

    @pl.when(source)
    def _():
        xk[...] = xq[pl.ds(4 * lax.rem(gc, 2), 4)]

    nodes_k = xk[...].reshape(64, 384)
    kv = dot(nodes_k[:, :256], wqkv_v[:, 256:]).astype(BF16).astype(F32)
    k_v[...] = kv[:, :256]
    v_v[...] = kv[:, 256:]
    km_v[...] = nodes_k[:, 256:].astype(F32)

    def s_copy(owner, slot, index):
        return pltpu.make_async_remote_copy(
            src_ref=stat.at[owner], dst_ref=rstat.at[slot], send_sem=sends.at[index],
            recv_sem=recvs.at[slot], device_id={"gc": owner}, device_id_type=MESH,
        )

    def owner_of(t):
        h = lax.div(t, 2)
        chip = lax.rem(lax.div(gc, 2) + 2 + h - lax.div(h, 2) * (2 * h - 1), 4)
        return 2 * chip + lax.rem(gc + t + 1, 2)

    def attend(t, carry):
        owner = owner_of(t)
        first = pl.multiple_of(owner * 16, 16)

        peak = jnp.full((16, 256), -3e38, F32)
        for j in range(64):
            live = jnp.broadcast_to(km_v[j : j + 1, :], (16, 128)) > 0
            live = jnp.concatenate([live, live], axis=1)
            k = jnp.broadcast_to(k_v[j : j + 1, :], (16, 256))
            s = k * film[j, pl.ds(first, 16), :256] + film[j, pl.ds(first, 16), 256:]
            s = jnp.where(live, s, NEG)
            score[j, pl.ds(first, 16), :] = s
            peak = jnp.maximum(peak, s)
        total = jnp.zeros((16, 256), F32)
        weighted = jnp.zeros((16, 256), F32)
        for j in range(64):
            v = jnp.broadcast_to(v_v[j : j + 1, :], (16, 256))
            p = jnp.exp2(score[j, pl.ds(first, 16), :] - peak)
            total = total + p
            weighted = weighted + p * v
        stat[owner, 0] = peak + jnp.log(total) * LOG2E
        stat[owner, 1] = weighted / total

        @pl.when(t >= 1)
        def _():
            s_copy(owner_of(t - 1), gc, t - 1).start()

        return carry

    lax.fori_loop(0, n_gc, attend, 0)

    gain1, gain2 = g1c[...], g2c[...]

    def message_stage(n):
        for h in range(2):
            m = 2 * n + h
            sb = (score[2 * m : 2 * m + 2].reshape(256, 256) * LN2).astype(BF16)
            u_s[m % 4] = e0[:, 256 * m : 256 * m + 256] + dot_nt(weo_v[...], sb)

    def norm_stage(n):
        for h in range(2):
            m = 2 * n + h
            for r in range(2):
                cols = slice(128 * r, 128 * r + 128)
                e_s[m % 8, :, cols] = (norm(u_s[m % 4, :, cols], 0) * gain1).astype(BF16)

    def up_stage(n):
        for h in range(2):
            m = 2 * n + h
            h_s[m % 4] = jnp.maximum(dot(weut[...], e_s[m % 8]).astype(BF16), 0.0)

    def down_stage(n):
        for h in range(2):
            m = 2 * n + h
            u = e_s[m % 8].astype(F32) + dot(wed_v[...], h_s[m % 4])
            for r in range(2):
                y = norm(u[:, 128 * r : 128 * r + 128], 0) * gain2
                yrow[(m // 8) % 2, pl.ds(2 * (m % 8) + r, 32, stride=16), :] = y
        if n % 4 == 3:
            at = 4 * n - 12
            keep = km_v[at : at + 16, :] * row_mask
            edge_v[:, at : at + 16, :] = (
                yrow[(n // 4) % 2].reshape(32, 16, 128) * keep[None]
            ).astype(BF16)

    for n in range(19):
        for lag, stage in enumerate((message_stage, norm_stage, up_stage, down_stage)):
            if 0 <= n - lag < 16:
                stage(n - lag)

    for i in range(13, 18):
        loads[i].wait()
    rstat[pl.ds(gc, 1)] = stat[pl.ds(gc, 1)]
    for t in range(1, n_gc):
        s_copy(gc, lax.rem(gc + t, n_gc), 0).wait_recv()
    peak = rstat[0, 0]
    for s in range(1, n_gc):
        peak = jnp.maximum(peak, rstat[s, 0])
    total = jnp.zeros((16, 256), F32)
    weighted = jnp.zeros((16, 256), F32)
    for s in range(n_gc):
        factor = jnp.exp2(rstat[s, 0] - peak)
        total = total + factor
        weighted = weighted + rstat[s, 1] * factor
    attn = (weighted / total).astype(BF16)
    own = send[...].astype(F32)
    n1 = (norm(own[:, :256] + dot(attn, wno_v[...]), 1) * ng1_v[...]).astype(BF16)
    hid = jnp.maximum(dot(n1, wnu_v[...]), 0.0).astype(BF16)
    n2 = norm(n1.astype(F32) + dot(hid, wnd_v[...]), 1) * ng2_v[...]
    node_v[...] = (n2 * jnp.concatenate([own[:, 256:]] * 2, axis=1)).astype(BF16)
    for copy in q_sent:
        copy.wait_send()

    @pl.when(source)
    def _():
        for t in range(12):
            k_copy(gr, 0, t).wait_send()

    for t in range(n_gc - 1):
        s_copy(gc, gc, t).wait_send()


def store(node_i, edge_i, node_o, edge_o, sem):
    copies = [
        pltpu.make_async_copy(edge_i, edge_o, sem.at[0]),
        pltpu.make_async_copy(node_i, node_o, sem.at[1]),
    ]
    for copy in copies:
        copy.start()
    for copy in copies:
        copy.wait()


def body(*args):
    (x_in, node_type, node_mask, adj, ori, ttab, atab, otab, wqkv, wfilm,
     weo, wno, wnu, wnd, weu, wed, ng1, ng2, eg1, eg2) = args
    args = (x_in, node_type, node_mask, adj, ori, ttab, atab, otab, wqkv, wfilm,
            weo.T, wno, wnu, wnd, weu, wed.T, ng1[None], ng2[None], eg1[None], eg2[None])
    anyspace = pl.BlockSpec(memory_space=pl.ANY)
    vmem = pl.BlockSpec(memory_space=pltpu.VMEM)
    hbm = pl.BlockSpec(memory_space=pltpu.HBM)
    V = pltpu.VMEM
    D = pltpu.SemaphoreType.DMA
    loaded = [args[0]] + list(args[3:])
    node, edge = pl.pallas_call(
        kernel,
        out_shape=(
            jax.ShapeDtypeStruct((16, 256), BF16),
            jax.ShapeDtypeStruct((32, 64, 128), BF16),
        ),
        in_specs=[hbm] * 20,
        out_specs=(vmem, vmem),
        scratch_shapes=[pltpu.SMEM((16,), jnp.int32)] * 2 + [V(a.shape, a.dtype) for a in loaded] + [
            V((16, 384), BF16),
            V((8, 16, 384), BF16),
            V((4, 16, 384), BF16),
            V((8, 2, 16, 256), F32),
            V((8, 2, 16, 256), F32),
            V((128, 128), F32),
            V((128, 512), F32),
            V((128, 512), BF16),
            V((32, 128), BF16),
            V((8, 128, 128), F32),
            V((1024, 128), BF16),
            V((64, 128, 512), F32),
            V((64, 128, 256), F32),
            V((32, 8192), F32),
            V((2, 512, 128), F32),
            V((128, 256), F32),
            V((64, 256), F32),
            V((64, 256), F32),
            V((64, 128), F32),
            V((128, 32), BF16),
            V((32, 128), F32),
            V((32, 128), F32),
            V((4, 32, 256), F32),
            V((8, 32, 256), BF16),
            V((4, 128, 256), BF16),
            D((20,)), D((7,)), D((8,)), D((12,)), D((4,)), D((7,)), D((8,)),
        ],
        compiler_params=pltpu.CompilerParams(
            collective_id=0, has_side_effects=True, vmem_limit_bytes=40 * 1024 * 1024
        ),
    )(*[pltpu.with_memory_space_constraint(a, pltpu.HBM) for a in args])
    return pl.pallas_call(
        store,
        out_shape=(
            jax.ShapeDtypeStruct((16, 256), BF16),
            jax.ShapeDtypeStruct((32, 64, 128), BF16),
        ),
        in_specs=[anyspace, anyspace],
        out_specs=(hbm, hbm),
        scratch_shapes=[D((2,))],
        compiler_params=pltpu.CompilerParams(vmem_limit_bytes=4 * 1024 * 1024),
    )(node, edge)


def solution(mesh):
    nodes = P(("graph", "gr", "gc"))
    rows = P(("graph", "gr", "gc"), None)
    pair = P(("graph", "gc"), "gr")
    return jax.shard_map(
        body,
        mesh=mesh,
        in_specs=(rows, nodes, nodes, pair, pair) + (P(),) * 15,
        out_specs=(rows, P(None, ("graph", "gc"), "gr")),
        check_vma=False,
    )
```

```python
import functools
import math

import jax
import jax.numpy as jnp
from jax import lax
from jax.experimental import pallas as pl
from jax.experimental.pallas import tpu as pltpu
from jax.sharding import PartitionSpec as P

MESH = pl.DeviceIdType.MESH
F32, BF16 = jnp.float32, jnp.bfloat16
HEAD_DIM = 32
LN2 = math.log(2.0)
LOG2E = math.log2(math.e)
NEG = -1000000000.0 * LOG2E
NT = (((1,), (1,)), ((), ()))


def dot(a, b):
    return jnp.dot(a, b, preferred_element_type=F32)


def dot_nt(a, b):
    return lax.dot_general(a, b, NT, preferred_element_type=F32)


def eye(n):
    rows = lax.broadcasted_iota(jnp.int32, (n, n), 0)
    cols = lax.broadcasted_iota(jnp.int32, (n, n), 1)
    return rows == cols


def norm(u, axis):
    center = u - jnp.mean(u, axis=axis, keepdims=True)
    spread = jnp.mean(center * center, axis=axis, keepdims=True)
    return center * lax.rsqrt(spread + 1e-05)


def kernel(
    x_h, type_h, mask_h, adj_h, ori_h, ttab_h, atab_h, otab_h, wqkv_h, wfilm_h,
    weo_h, wno_h, wnu_h, wnd_h, weu_h, wed_h, ng1_h, ng2_h, eg1_h, eg2_h,
    node_v, edge_v,
    type_s, mask_s,
    x_v, adj_v, ori_v, ttab_v, atab_v, otab_v, wqkv_v, wfilm_v,
    weo_v, wno_v, wnu_v, wnd_v, weu_v, wed_v, ng1_v, ng2_v, eg1_v, eg2_v,
    send, xq, xk, stat, rstat,
    t40, ft32, ftab, t40t, codes, onehot, film, score, e0, yrow,
    q_v, k_v, v_v, km_v, weut, g1c, g2c, u_s, e_s, h_s,
    in_sem, sendq, recvq, sendk, recvk, sends, recvs,
):
    gr, gc = lax.axis_index("gr"), lax.axis_index("gc")
    n_gr, n_gc = 4, 8

    barrier = pltpu.get_barrier_semaphore()
    home = lax.div(gc, 2)
    source = home == gr

    @pl.when(jnp.logical_not(source))
    def _():
        pl.semaphore_signal(barrier, inc=1, device_id={"gr": home}, device_id_type=MESH)

    for t in range(1, n_gc):
        pl.semaphore_signal(
            barrier, inc=1, device_id={"gc": lax.rem(gc + t, n_gc)}, device_id_type=MESH
        )
    pairs = [
        (x_h, x_v), (ttab_h, ttab_v), (adj_h, adj_v), (ori_h, ori_v),
        (atab_h, atab_v), (otab_h, otab_v), (wfilm_h, wfilm_v), (wqkv_h, wqkv_v),
        (weo_h, weo_v), (weu_h, weu_v), (wed_h, wed_v), (eg1_h, eg1_v), (eg2_h, eg2_v),
        (wno_h, wno_v), (wnu_h, wnu_v), (wnd_h, wnd_v), (ng1_h, ng1_v), (ng2_h, ng2_v),
        (type_h, type_s), (mask_h, mask_s),
    ]
    loads = [pltpu.make_async_copy(a, b, in_sem.at[i]) for i, (a, b) in enumerate(pairs)]
    for i in [18, 19] + list(range(18)):
        loads[i].start()

    for i in (18, 19, 0, 1):
        loads[i].wait()
    row_id = lax.broadcasted_iota(jnp.int32, (16, 256), 0)
    embedded = jnp.zeros((16, 256), F32)
    valid = jnp.zeros((16, 128), F32)
    for r in range(16):
        line = ttab_v[pl.ds(type_s[r], 1), :]
        embedded = jnp.where(row_id == r, line, embedded)
        valid = jnp.where(row_id[:, :128] == r, mask_s[r].astype(F32), valid)
    send[:, :256] = (x_v[...].astype(F32) + embedded).astype(BF16)
    send[:, 256:] = valid.astype(BF16)
    xq[pl.ds(gc, 1)] = send[...][None]

    def q_copy(peer, slot, index):
        return pltpu.make_async_remote_copy(
            src_ref=send, dst_ref=xq.at[slot], send_sem=sendq.at[index],
            recv_sem=recvq.at[slot], device_id={"gc": peer}, device_id_type=MESH,
        )

    def k_copy(peer, slot, index):
        return pltpu.make_async_remote_copy(
            src_ref=xq.at[4 * lax.rem(gc, 2) + slot], dst_ref=xk.at[slot], send_sem=sendk.at[index],
            recv_sem=recvk.at[slot], device_id={"gr": peer}, device_id_type=MESH,
        )

    @pl.when(source)
    def _():
        pl.semaphore_wait(barrier, n_gc - 1 + n_gr - 1)

    @pl.when(jnp.logical_not(source))
    def _():
        pl.semaphore_wait(barrier, n_gc - 1)

    q_sent = [q_copy(lax.rem(gc + t, n_gc), gc, t - 1) for t in (4, 3, 5, 2, 6, 1, 7)]
    for copy in q_sent:
        copy.start()
    for t in range(1, n_gc):
        @pl.when(source)
        def _():
            q_copy(gc, lax.rem(gc + t, n_gc), 0).wait_recv()

    @pl.when(source)
    def _():
        for t in (2, 1, 3):
            for slot in range(4):
                k_copy(lax.rem(gr + t, n_gr), slot, 3 * slot + t - 1).start()

    loads[4].wait()
    loads[5].wait()
    loads[6].wait()
    t40[...] = jnp.zeros_like(t40)
    ft32[...] = jnp.zeros_like(ft32)
    for a in range(5):
        t40[8 * a : 8 * a + 8, :32] = atab_v[a : a + 1, :] + otab_v[...]
    table = t40[...].astype(BF16)
    values = dot(table[:40, :32], wfilm_v[...])
    lane = lax.broadcasted_iota(jnp.int32, (40, 512), 1)
    values = values + jnp.where(lane < 256, 1.0, 0.0)
    values = values * LOG2E
    high = values.astype(BF16).astype(F32)
    middle = (values - high).astype(BF16).astype(F32)
    ft32[0:40] = high
    ft32[40:80] = middle
    ft32[80:120] = values - high - middle
    ftab[...] = ft32[...].astype(BF16)
    t40t[...] = t40[...].T[:32].astype(BF16)

    loads[2].wait()
    loads[3].wait()
    code = (adj_v[...] * 8 + ori_v[...]).astype(F32)
    code_t = jnp.concatenate([code, code], axis=0).T
    for b in range(8):
        codes[b] = pltpu.roll(code_t, (128 - 8 * b) % 128, 1)
    lane = lax.broadcasted_iota(jnp.int32, (128, 128), 1)
    label = jnp.where(lane < 40, lane, jnp.where(lane < 80, lane - 40, lane - 80))
    label = jnp.where(lane < 120, label, -1).astype(F32)

    def film_block(b, carry):
        block = codes[b]
        for r in range(8):
            hit = jnp.broadcast_to(block[:, r : r + 1], (128, 128)) == label
            onehot[128 * r : 128 * r + 128] = jnp.where(hit, 1.0, 0.0).astype(BF16)
        hot = onehot[...]
        film[pl.ds(b * 8, 8)] = dot(hot, ftab[...]).reshape(8, 128, 512)
        e0[:, pl.ds(pl.multiple_of(b * 1024, 1024), 1024)] = dot_nt(t40t[...], hot)
        return carry

    lax.fori_loop(0, 8, film_block, 0)

    for i in range(8, 13):
        loads[i].wait()
    weut[...] = weu_v[...].astype(F32).T.astype(BF16)
    for g_ref, c_ref in ((eg1_v, g1c), (eg2_v, g2c)):
        spread = jnp.where(eye(32), jnp.broadcast_to(g_ref[...], (32, 32)), 0.0)
        c_ref[...] = jnp.broadcast_to(jnp.sum(spread, axis=1, keepdims=True), (32, 128))

    for t in range(1, n_gc):
        @pl.when(jnp.logical_not(source))
        def _():
            q_copy(gc, lax.rem(gc + t, n_gc), 0).wait_recv()

    loads[7].wait()
    nodes_q = xq[...].reshape(128, 384)
    q = dot(nodes_q[:, :256], wqkv_v[:, :256]).astype(BF16)
    q_v[...] = q.astype(F32) * (1.0 / math.sqrt(HEAD_DIM))
    row_mask = nodes_q[:, 256:].astype(F32).T[0:1, :]

    def scale_block(b, carry):
        rows = pl.ds(pl.multiple_of(b * 16, 16), 16)
        qs = q_v[rows, :]
        for j in range(64):
            film[j, rows, :256] = film[j, rows, :256] * qs
        return carry

    lax.fori_loop(0, 8, scale_block, 0)

    @pl.when(jnp.logical_not(source))
    def _():
        for t in range(4):
            k_copy(gr, t, 0).wait_recv()

    @pl.when(source)
    def _():
        xk[...] = xq[pl.ds(4 * lax.rem(gc, 2), 4)]

    nodes_k = xk[...].reshape(64, 384)
    kv = dot(nodes_k[:, :256], wqkv_v[:, 256:]).astype(BF16).astype(F32)
    k_v[...] = kv[:, :256]
    v_v[...] = kv[:, 256:]
    km_v[...] = nodes_k[:, 256:].astype(F32)

    def s_copy(owner, slot, index):
        return pltpu.make_async_remote_copy(
            src_ref=stat.at[owner], dst_ref=rstat.at[slot], send_sem=sends.at[index],
            recv_sem=recvs.at[slot], device_id={"gc": owner}, device_id_type=MESH,
        )

    def owner_of(t):
        h = lax.div(t, 2)
        chip = lax.rem(lax.div(gc, 2) + 2 + h - lax.div(h, 2) * (2 * h - 1), 4)
        return 2 * chip + lax.rem(gc + t + 1, 2)

    def attend(t, carry):
        owner = owner_of(t)
        first = pl.multiple_of(owner * 16, 16)

        peak = jnp.full((16, 256), -3e38, F32)
        for j in range(64):
            live = jnp.broadcast_to(km_v[j : j + 1, :], (16, 128)) > 0
            live = jnp.concatenate([live, live], axis=1)
            k = jnp.broadcast_to(k_v[j : j + 1, :], (16, 256))
            s = k * film[j, pl.ds(first, 16), :256] + film[j, pl.ds(first, 16), 256:]
            s = jnp.where(live, s, NEG)
            score[j, pl.ds(first, 16), :] = s
            peak = jnp.maximum(peak, s)
        total = jnp.zeros((16, 256), F32)
        weighted = jnp.zeros((16, 256), F32)
        for j in range(64):
            v = jnp.broadcast_to(v_v[j : j + 1, :], (16, 256))
            p = jnp.exp2(score[j, pl.ds(first, 16), :] - peak)
            total = total + p
            weighted = weighted + p * v
        stat[owner, 0] = peak + jnp.log(total) * LOG2E
        stat[owner, 1] = weighted / total

        @pl.when(t >= 1)
        def _():
            s_copy(owner_of(t - 1), gc, t - 1).start()

        return carry

    lax.fori_loop(0, n_gc, attend, 0)

    gain1, gain2 = g1c[...], g2c[...]

    def message_stage(n):
        for h in range(2):
            m = 2 * n + h
            sb = (score[2 * m : 2 * m + 2].reshape(256, 256) * LN2).astype(BF16)
            u_s[m % 4] = e0[:, 256 * m : 256 * m + 256] + dot_nt(weo_v[...], sb)

    def norm_stage(n):
        for h in range(2):
            m = 2 * n + h
            for r in range(2):
                cols = slice(128 * r, 128 * r + 128)
                e_s[m % 8, :, cols] = (norm(u_s[m % 4, :, cols], 0) * gain1).astype(BF16)

    def up_stage(n):
        for h in range(2):
            m = 2 * n + h
            h_s[m % 4] = jnp.maximum(dot(weut[...], e_s[m % 8]).astype(BF16), 0.0)

    def down_stage(n):
        for h in range(2):
            m = 2 * n + h
            u = e_s[m % 8].astype(F32) + dot(wed_v[...], h_s[m % 4])
            for r in range(2):
                y = norm(u[:, 128 * r : 128 * r + 128], 0) * gain2
                yrow[(m // 8) % 2, pl.ds(2 * (m % 8) + r, 32, stride=16), :] = y
        if n % 4 == 3:
            at = 4 * n - 12
            keep = km_v[at : at + 16, :] * row_mask
            edge_v[:, at : at + 16, :] = (
                yrow[(n // 4) % 2].reshape(32, 16, 128) * keep[None]
            ).astype(BF16)

    for n in range(19):
        for lag, stage in enumerate((message_stage, norm_stage, up_stage, down_stage)):
            if 0 <= n - lag < 16:
                stage(n - lag)

    for i in range(13, 18):
        loads[i].wait()
    rstat[pl.ds(gc, 1)] = stat[pl.ds(gc, 1)]
    for t in range(1, n_gc):
        s_copy(gc, lax.rem(gc + t, n_gc), 0).wait_recv()
    peak = rstat[0, 0]
    for s in range(1, n_gc):
        peak = jnp.maximum(peak, rstat[s, 0])
    total = jnp.zeros((16, 256), F32)
    weighted = jnp.zeros((16, 256), F32)
    for s in range(n_gc):
        factor = jnp.exp2(rstat[s, 0] - peak)
        total = total + factor
        weighted = weighted + rstat[s, 1] * factor
    attn = (weighted / total).astype(BF16)
    own = send[...].astype(F32)
    n1 = (norm(own[:, :256] + dot(attn, wno_v[...]), 1) * ng1_v[...]).astype(BF16)
    hid = jnp.maximum(dot(n1, wnu_v[...]), 0.0).astype(BF16)
    n2 = norm(n1.astype(F32) + dot(hid, wnd_v[...]), 1) * ng2_v[...]
    node_v[...] = (n2 * jnp.concatenate([own[:, 256:]] * 2, axis=1)).astype(BF16)
    for copy in q_sent:
        copy.wait_send()

    @pl.when(source)
    def _():
        for t in range(12):
            k_copy(gr, 0, t).wait_send()

    for t in range(n_gc - 1):
        s_copy(gc, gc, t).wait_send()


def store(node_i, edge_i, node_o, edge_o, sem):
    copies = [
        pltpu.make_async_copy(edge_i, edge_o, sem.at[0]),
        pltpu.make_async_copy(node_i, node_o, sem.at[1]),
    ]
    for copy in copies:
        copy.start()
    for copy in copies:
        copy.wait()


def body(*args):
    (x_in, node_type, node_mask, adj, ori, ttab, atab, otab, wqkv, wfilm,
     weo, wno, wnu, wnd, weu, wed, ng1, ng2, eg1, eg2) = args
    args = (x_in, node_type, node_mask, adj, ori, ttab, atab, otab, wqkv, wfilm,
            weo.T, wno, wnu, wnd, weu, wed.T, ng1[None], ng2[None], eg1[None], eg2[None])
    anyspace = pl.BlockSpec(memory_space=pl.ANY)
    vmem = pl.BlockSpec(memory_space=pltpu.VMEM)
    hbm = pl.BlockSpec(memory_space=pltpu.HBM)
    V = pltpu.VMEM
    D = pltpu.SemaphoreType.DMA
    loaded = [args[0]] + list(args[3:])
    node, edge = pl.pallas_call(
        kernel,
        out_shape=(
            jax.ShapeDtypeStruct((16, 256), BF16),
            jax.ShapeDtypeStruct((32, 64, 128), BF16),
        ),
        in_specs=[hbm] * 20,
        out_specs=(vmem, vmem),
        scratch_shapes=[pltpu.SMEM((16,), jnp.int32)] * 2 + [V(a.shape, a.dtype) for a in loaded] + [
            V((16, 384), BF16),
            V((8, 16, 384), BF16),
            V((4, 16, 384), BF16),
            V((8, 2, 16, 256), F32),
            V((8, 2, 16, 256), F32),
            V((128, 128), F32),
            V((128, 512), F32),
            V((128, 512), BF16),
            V((32, 128), BF16),
            V((8, 128, 128), F32),
            V((1024, 128), BF16),
            V((64, 128, 512), F32),
            V((64, 128, 256), F32),
            V((32, 8192), F32),
            V((2, 512, 128), F32),
            V((128, 256), F32),
            V((64, 256), F32),
            V((64, 256), F32),
            V((64, 128), F32),
            V((128, 32), BF16),
            V((32, 128), F32),
            V((32, 128), F32),
            V((4, 32, 256), F32),
            V((8, 32, 256), BF16),
            V((4, 128, 256), BF16),
            D((20,)), D((7,)), D((8,)), D((12,)), D((4,)), D((7,)), D((8,)),
        ],
        compiler_params=pltpu.CompilerParams(
            collective_id=0, has_side_effects=True, vmem_limit_bytes=40 * 1024 * 1024
        ),
    )(*[pltpu.with_memory_space_constraint(a, pltpu.HBM) for a in args])
    return pl.pallas_call(
        store,
        out_shape=(
            jax.ShapeDtypeStruct((16, 256), BF16),
            jax.ShapeDtypeStruct((32, 64, 128), BF16),
        ),
        in_specs=[anyspace, anyspace],
        out_specs=(hbm, hbm),
        scratch_shapes=[D((2,))],
        compiler_params=pltpu.CompilerParams(vmem_limit_bytes=4 * 1024 * 1024),
    )(node, edge)


def solution(mesh):
    nodes = P(("graph", "gr", "gc"))
    rows = P(("graph", "gr", "gc"), None)
    pair = P(("graph", "gc"), "gr")
    return jax.shard_map(
        body,
        mesh=mesh,
        in_specs=(rows, nodes, nodes, pair, pair) + (P(),) * 15,
        out_specs=(rows, P(None, ("graph", "gc"), "gr")),
        check_vma=False,
    )
```
